32 devices in a mesh: sample: 4 (over z), tensor: 2 (over y), section: 4 (over x, core).
Axes of the slice: x: 2, y: 2, z: 4, core: 2. Of those that a mesh axis runs over, the one named last changes fastest.
Arguments:
- hidden_in: bfloat16 [512, 8192], P('sample', 'section'), may hold values from -6 to 6
- token_ids: int32 [512], P('sample'), may hold values from 0 to 128255, as said below
- mlp_gain: bfloat16 [8192], P('section'), may hold values from 0.099609375 to 1.8984375
- attn_gain: bfloat16 [8192], P('section'), may hold values from 0.099609375 to 1.8984375
- gate_weight: bfloat16 [28672, 8192], P(('sample', 'tensor'), 'section'), may hold values from -0.0625 to 0.0625
- up_weight: bfloat16 [28672, 8192], P(('sample', 'tensor'), 'section'), may hold values from -0.0625 to 0.0625
- down_weight: bfloat16 [28672, 8192], P(('sample', 'tensor'), 'section'), may hold values from -0.03125 to 0.03125
Outputs:
- hidden_out: bfloat16 [512, 8192], P('sample', 'section')
- mlp_cov: float32 [8192, 8192], P('section', ('sample', 'tensor'))
- attn_cov: float32 [8192, 8192], P('section', ('sample', 'tensor'))
The draws below stay inside these ranges and needn't reach their ends.
Inputs may be any that keep to these rules, and one draw needn't show every extreme that they name: `token_ids`: 0 is padding and is left out of the statistics; within each block of 128 rows the padding forms the tail, and the last block has none.
All inputs are finite; a program needn't handle non-finite values.
Results may differ from the reference program's by a relative error of at most 0.0071.
Values may be sent and summed in bfloat16 or wider, within the bound.
A program may use at most 256 MiB of HBM per device.

```python
import jax
import jax.numpy as jnp
from jax import lax

D = 8192
FF = 28672
VOCAB = 128256
TOK_DEV = 128
TOKENS = 512
N_SAMPLE = 4


def draw_token_ids(key, part):
    key_jitter = jax.random.fold_in(key, 11)
    key_ids = jax.random.fold_in(key, 23)
    block_index = jnp.arange(N_SAMPLE)
    base_length = TOK_DEV // 4 + (TOK_DEV - TOK_DEV // 4) * block_index // (N_SAMPLE - 1)
    jitter = jax.random.randint(key_jitter, (N_SAMPLE,), 0, TOK_DEV // 8 + 1)
    jitter = jnp.where(block_index == N_SAMPLE - 1, 0, jitter)
    lengths = jnp.maximum(base_length - jitter, 1)
    positions = jnp.arange(TOKENS)
    within = positions % TOK_DEV
    blocks = positions // TOK_DEV
    live = within < lengths[blocks]
    tokens_drawn = jax.random.randint(key_ids, (TOKENS,), 1, VOCAB)
    return jnp.where(live, tokens_drawn, 0).astype(jnp.int32)


def steps_of(rng, dims, pieces, low, largest):
    def one(position, parts):
        steps = jax.random.uniform(jax.random.fold_in(jax.random.fold_in(rng, 6), position), (parts,), jnp.float32, low / len(pieces), largest / len(pieces))
        return jnp.repeat(jnp.exp(steps), dims[position] // parts).reshape((-1,) + (1,) * (len(dims) - position - 1))

    factor_of = one(*pieces[0])
    for cut in pieces[1:]:
        factor_of = factor_of * one(*cut)
    return factor_of


def scatter_about(own_key, dims, scale, bound, split=(), kind=jnp.bfloat16):
    result = scale * jax.random.normal(own_key, dims, jnp.float32)
    if split:
        result = result * steps_of(own_key, dims, split, -0.22, 0.18)
    return jnp.clip(result, -bound, bound).astype(kind)


def setup_inputs(seed: int = 0) -> dict:
    arg_keys = jax.random.split(jax.random.key(seed), 8)
    return {
        "hidden_in": scatter_about(arg_keys[0], (TOKENS, D), 1.0, 6.0, ((0, 4), (1, 4))),
        "token_ids": draw_token_ids(jax.random.fold_in(arg_keys[7], 71), 0),
        "mlp_gain": jnp.clip(1.0 + 0.18 * jax.random.normal(arg_keys[2], (D,), jnp.float32), 0.099609375, 1.8984375).astype(jnp.bfloat16),
        "attn_gain": jnp.clip(1.0 + 0.18 * jax.random.normal(arg_keys[3], (D,), jnp.float32), 0.099609375, 1.8984375).astype(jnp.bfloat16),
        "gate_weight": scatter_about(arg_keys[4], (FF, D), D ** -0.5, 0.0625, ((0, 8), (1, 4))),
        "up_weight": scatter_about(arg_keys[5], (FF, D), D ** -0.5, 0.0625, ((0, 8), (1, 4))),
        "down_weight": scatter_about(arg_keys[6], (FF, D), FF ** -0.5, 0.03125, ((0, 8), (1, 4))),
    }


EPS = 1e-05

def rms_norm(values_in, gain):
    values = values_in.astype(jnp.float32)
    totals = lax.optimization_barrier(jnp.sum(values * values, axis=1))
    scales = lax.rsqrt(totals / D + EPS)
    return (values * scales[:, None] * gain.astype(jnp.float32)).astype(jnp.bfloat16)

def covariance(rows_in, live, live_count):
    weighted = rows_in * live[:, None]
    products = jnp.dot(weighted.T, rows_in, preferred_element_type=jnp.float32)
    means = jnp.dot(live, rows_in, preferred_element_type=jnp.float32) / live_count
    return products / live_count - means[:, None] * means[None, :]

def reference(hidden_in, token_ids, mlp_gain, attn_gain, gate_weight, up_weight, down_weight):
    live = (token_ids != 0).astype(jnp.bfloat16)
    live_count = jnp.sum(live.astype(jnp.float32))
    mlp_input = rms_norm(hidden_in, mlp_gain)
    gate_sum = jnp.dot(mlp_input, gate_weight.T, preferred_element_type=jnp.float32)
    up_sum = jnp.dot(mlp_input, up_weight.T, preferred_element_type=jnp.float32)
    hidden_units = (jax.nn.silu(gate_sum) * up_sum).astype(jnp.bfloat16)
    update = jnp.dot(hidden_units, down_weight, preferred_element_type=jnp.float32)
    hidden_out = (hidden_in.astype(jnp.float32) + update).astype(jnp.bfloat16)
    attn_input = rms_norm(hidden_out, attn_gain)
    mlp_cov = covariance(mlp_input, live, live_count)
    attn_cov = covariance(attn_input, live, live_count)
    return (hidden_out, mlp_cov, attn_cov)
```

```python
import jax
import jax.numpy as jnp
from jax import lax
from jax.sharding import PartitionSpec as P

EPS = 1e-05
CHUNKS = 2
ROW_CONTRACT = (((1,), (1,)), ((), ()))
TOKEN_CONTRACT = (((0,), (0,)), ((), ()))
F32 = jnp.float32
BF16 = jnp.bfloat16


def swap(x, axis, d):
    return lax.ppermute(x, axis, [(i, i ^ d) for i in range(lax.axis_size(axis))])


def bits_up(axis):
    n, d, out = lax.axis_size(axis), 1, []
    while d < n:
        out.append(d)
        d *= 2
    return out


def offsets(axis):
    order = [0]
    for d in reversed(bits_up(axis)):
        order = order + [o ^ d for o in order]
    return order


def butterfly(x, axis):
    for d in bits_up(axis):
        x = x + swap(x, axis, d)
    return x


def doubled(x, axis):
    for d in reversed(bits_up(axis)):
        x = jnp.concatenate([x, swap(x, axis, d)], axis=0)
    return x


def halved(x, axis):
    for d in bits_up(axis):
        half = x.shape[0] // 2
        got = swap(x[half:].astype(BF16), axis, d)
        x = x[:half].astype(F32) + got.astype(F32)
    return x


def columns_of(rows, start, width, owners):
    names = ("sample", "tensor", "section")
    n_section = lax.axis_size("section")
    me = lax.axis_index("section")
    group = lax.axis_index("sample") * lax.axis_size("tensor") + lax.axis_index("tensor")
    owner = group * n_section // len(owners)
    value = lax.dynamic_slice_in_dim(rows, start, width, 1)
    have = [0]
    for d in reversed(bits_up("section")):
        pairs = [
            (g * n_section + (o ^ h), g * n_section + (o ^ h ^ d))
            for g, o in enumerate(owners)
            for h in have
        ]
        got = lax.ppermute(value, names, pairs)
        rel = me ^ owner
        takes = jnp.zeros((), jnp.bool_)
        for h in have:
            takes = takes | (rel == (h ^ d))
        value = jnp.where(takes, got, value)
        have = have + [h ^ d for h in have]
    return value


def normed(values, totals, gain, width):
    scales = lax.rsqrt(totals / width + EPS)
    return (values.astype(F32) * scales[:, None] * gain.astype(F32)).astype(BF16)


def covariance(rows_in, columns, live, count):
    weighted = rows_in * live[:, None]
    products = lax.dot_general(weighted, columns, TOKEN_CONTRACT, preferred_element_type=F32)
    row_means = jnp.dot(live, rows_in, preferred_element_type=F32) / count
    col_means = jnp.dot(live, columns, preferred_element_type=F32) / count
    return products / count - row_means[:, None] * col_means[None, :]


def local(hidden_in, token_ids, mlp_gain, attn_gain, gate_weight, up_weight, down_weight):
    n_sample = lax.axis_size("sample")
    n_tensor = lax.axis_size("tensor")
    n_section = lax.axis_size("section")
    tok_local, panel = hidden_in.shape
    width = panel * n_section
    share = tok_local // n_tensor
    groups = n_sample * n_tensor
    col_width = width // groups
    owners = [g * n_section // groups for g in range(groups)]
    t = lax.axis_index("tensor")
    c = lax.axis_index("section")
    group = lax.axis_index("sample") * n_tensor + t
    col_start = group * col_width - group * n_section // groups * panel
    t_order = offsets("tensor")
    q_order = offsets("section")

    def relative(x, order, me, size):
        return [lax.dynamic_slice_in_dim(x, (me ^ o) * size, size, 0) for o in order]

    values = hidden_in.astype(F32)
    totals = butterfly(jnp.sum(values * values, axis=1), "section")
    flags = jnp.stack([totals, (token_ids != 0).astype(F32)], axis=1)
    mine = relative(hidden_in, t_order, t, share)
    flags_mine = jnp.concatenate(relative(flags, t_order, t, share), axis=0)
    raw, info = [jnp.concatenate(mine, axis=0)], [flags_mine]
    for j in range(1, n_sample):
        info.append(swap(flags_mine, "sample", j))
        raw.append(doubled(swap(mine[0], "sample", j), "tensor"))
    blocks = [normed(r, i[:, 0], mlp_gain, width) for r, i in zip(raw, info)]
    live = jnp.concatenate([i[:, 1] for i in info], axis=0)
    count = jnp.sum(live)
    live = live.astype(BF16)

    per = n_sample // CHUNKS
    own_sum = None
    for k in range(CHUNKS):
        rows = jnp.concatenate(blocks[k * per : (k + 1) * per], axis=0)
        part = rows.shape[0] // n_section
        ordered = jnp.concatenate(relative(rows, q_order, c, part), axis=0)
        gate = lax.dot_general(ordered, gate_weight, ROW_CONTRACT, preferred_element_type=F32)
        gate = halved(gate.astype(BF16), "section")
        up = lax.dot_general(ordered, up_weight, ROW_CONTRACT, preferred_element_type=F32)
        up = halved(up.astype(BF16), "section")
        units = (jax.nn.silu(gate) * up).astype(BF16)
        units = doubled(units, "section")
        hidden = jnp.zeros_like(units)
        for i, o in enumerate(q_order):
            piece = units[i * part : (i + 1) * part]
            hidden = lax.dynamic_update_slice_in_dim(hidden, piece, (c ^ o) * part, 0)
        update = jnp.dot(hidden, down_weight, preferred_element_type=F32)
        for i in range(per):
            j = k * per + i
            partial = halved(update[i * tok_local : (i + 1) * tok_local], "tensor")
            if j:
                partial = swap(partial.astype(BF16), "sample", j).astype(F32)
            own_sum = partial if own_sum is None else own_sum + partial

    updated = (mine[0].astype(F32) + own_sum).astype(BF16)
    out_values = updated.astype(F32)
    out_totals = butterfly(jnp.sum(out_values * out_values, axis=1), "section")

    mlp_rows = jnp.concatenate(blocks, axis=0)
    mlp_columns = columns_of(mlp_rows, col_start, col_width, owners)
    mlp_cov = covariance(mlp_rows, mlp_columns, live, count)

    attn_raw, attn_totals = [], []
    out_totals = doubled(out_totals[:, None], "tensor")
    for j in range(n_sample):
        block = swap(updated, "sample", j) if j else updated
        attn_raw.append(doubled(block, "tensor"))
        attn_totals.append(swap(out_totals, "sample", j) if j else out_totals)
    hidden_out = jnp.zeros_like(hidden_in)
    for i, o in enumerate(t_order):
        piece = attn_raw[0][i * share : (i + 1) * share]
        hidden_out = lax.dynamic_update_slice_in_dim(hidden_out, piece, (t ^ o) * share, 0)
    attn_rows = jnp.concatenate(
        [normed(r, i[:, 0], attn_gain, width) for r, i in zip(attn_raw, attn_totals)], axis=0
    )
    attn_columns = columns_of(attn_rows, col_start, col_width, owners)
    attn_cov = covariance(attn_rows, attn_columns, live, count)
    return (hidden_out, mlp_cov, attn_cov)


def solution(mesh):
    in_specs = (
        P("sample", "section"),
        P("sample"),
        P("section"),
        P("section"),
        P(("sample", "tensor"), "section"),
        P(("sample", "tensor"), "section"),
        P(("sample", "tensor"), "section"),
    )
    out_specs = (
        P("sample", "section"),
        P("section", ("sample", "tensor")),
        P("section", ("sample", "tensor")),
    )
    return jax.shard_map(local, mesh=mesh, in_specs=in_specs, out_specs=out_specs, check_vma=False)
```

```python
import jax
import jax.numpy as jnp
from jax import lax
from jax.experimental import pallas as pl
from jax.experimental.pallas import tpu as pltpu
from jax.sharding import PartitionSpec as P

EPS = 1e-05
CHUNKS = 2
ROW_CONTRACT = (((1,), (1,)), ((), ()))
TOKEN_CONTRACT = (((0,), (0,)), ((), ()))
F32 = jnp.float32
BF16 = jnp.bfloat16


def swap(x, axis, d):
    return lax.ppermute(x, axis, [(i, i ^ d) for i in range(lax.axis_size(axis))])


def bits_up(axis):
    n, d, out = lax.axis_size(axis), 1, []
    while d < n:
        out.append(d)
        d *= 2
    return out


def offsets(axis):
    order = [0]
    for d in reversed(bits_up(axis)):
        order = order + [o ^ d for o in order]
    return order


def butterfly(x, axis):
    for d in bits_up(axis):
        x = x + swap(x, axis, d)
    return x


def doubled(x, axis):
    for d in reversed(bits_up(axis)):
        x = jnp.concatenate([x, swap(x, axis, d)], axis=0)
    return x


def halved(x, axis, skip=0):
    for d in bits_up(axis)[skip:]:
        half = x.shape[0] // 2
        x = x[:half] + swap(x[half:].astype(BF16), axis, d).astype(F32)
    return x


def gate_up_kernel(rows_ref, gate_ref, up_ref, gate_keep, gate_send, up_keep, up_send):
    half = gate_keep.shape[0]
    for weight, keep, send in ((gate_ref, gate_keep, gate_send), (up_ref, up_keep, up_send)):
        out = lax.dot_general(
            rows_ref[...], weight[...], ROW_CONTRACT, preferred_element_type=F32
        )
        keep[...] = out[:half]
        send[...] = out[half:].astype(BF16)


def gate_up(rows, gate_weight, up_weight):
    n, depth = rows.shape
    units = gate_weight.shape[0]
    tile = next((k for k in (256, 128) if units % k == 0), units)
    half = n // 2
    weight_spec = pl.BlockSpec((tile, depth), lambda i: (i, 0))
    out_spec = pl.BlockSpec((half, tile), lambda i: (0, i))
    return pl.pallas_call(
        gate_up_kernel,
        grid=(units // tile,),
        in_specs=[pl.BlockSpec((n, depth), lambda i: (0, 0)), weight_spec, weight_spec],
        out_specs=[out_spec] * 4,
        out_shape=[
            jax.ShapeDtypeStruct((half, units), k) for k in (F32, BF16, F32, BF16)
        ],
        compiler_params=pltpu.CompilerParams(dimension_semantics=("arbitrary",)),
        cost_estimate=pl.CostEstimate(
            flops=4 * n * depth * units,
            bytes_accessed=4 * depth * units + 2 * n * depth + 6 * n * units,
            transcendentals=0,
        ),
    )(rows, gate_weight, up_weight)


def columns_of(rows, start, width, owners):
    names = ("sample", "tensor", "section")
    n_section = lax.axis_size("section")
    me = lax.axis_index("section")
    group = lax.axis_index("sample") * lax.axis_size("tensor") + lax.axis_index("tensor")
    owner = group * n_section // len(owners)
    value = lax.dynamic_slice_in_dim(rows, start, width, 1)
    have = [0]
    for d in reversed(bits_up("section")):
        pairs = [
            (g * n_section + (o ^ h), g * n_section + (o ^ h ^ d))
            for g, o in enumerate(owners)
            for h in have
        ]
        got = lax.ppermute(value, names, pairs)
        rel = me ^ owner
        takes = jnp.zeros((), jnp.bool_)
        for h in have:
            takes = takes | (rel == (h ^ d))
        value = jnp.where(takes, got, value)
        have = have + [h ^ d for h in have]
    return value


def normed(values, totals, gain, width):
    scales = lax.rsqrt(totals / width + EPS)
    return (values.astype(F32) * scales[:, None] * gain.astype(F32)).astype(BF16)


def covariance(rows_in, columns, live, count):
    weighted = rows_in * live[:, None]
    products = lax.dot_general(weighted, columns, TOKEN_CONTRACT, preferred_element_type=F32)
    row_means = jnp.dot(live, rows_in, preferred_element_type=F32) / count
    col_means = jnp.dot(live, columns, preferred_element_type=F32) / count
    return products / count - row_means[:, None] * col_means[None, :]


def local(hidden_in, token_ids, mlp_gain, attn_gain, gate_weight, up_weight, down_weight):
    n_sample = lax.axis_size("sample")
    n_tensor = lax.axis_size("tensor")
    n_section = lax.axis_size("section")
    tok_local, panel = hidden_in.shape
    width = panel * n_section
    share = tok_local // n_tensor
    groups = n_sample * n_tensor
    col_width = width // groups
    owners = [g * n_section // groups for g in range(groups)]
    t = lax.axis_index("tensor")
    c = lax.axis_index("section")
    group = lax.axis_index("sample") * n_tensor + t
    col_start = group * col_width - group * n_section // groups * panel
    t_order = offsets("tensor")
    q_order = offsets("section")

    def relative(x, order, me, size):
        return [lax.dynamic_slice_in_dim(x, (me ^ o) * size, size, 0) for o in order]

    values = hidden_in.astype(F32)
    totals = butterfly(jnp.sum(values * values, axis=1), "section")
    flags = jnp.stack([totals, (token_ids != 0).astype(F32)], axis=1)
    mine = relative(hidden_in, t_order, t, share)
    flags_mine = jnp.concatenate(relative(flags, t_order, t, share), axis=0)

    def gathered(x):
        out = [x]
        for j in range(1, n_sample):
            low = j & -j
            out.append(swap(out[j ^ low], "sample", low))
        return out

    order = list(range(0, n_sample, 2)) + list(range(1, n_sample, 2))
    info = gathered(flags_mine)
    raw = [jnp.concatenate(mine, axis=0)]
    raw += [doubled(r, "tensor") for r in gathered(mine[0])[1:]]
    raw = [raw[j] for j in order]
    info = [info[j] for j in order]
    live = jnp.concatenate([i[:, 1] for i in info], axis=0)
    count = jnp.sum(live)
    live = live.astype(BF16)

    per = n_sample // CHUNKS
    blocks, shares, after = [], [], ()
    for k in range(CHUNKS):
        held = (raw[k * per : (k + 1) * per], info[k * per : (k + 1) * per])
        held, after = lax.optimization_barrier((held, after))
        if after:
            shares.append(after)
        chunk = [normed(r, i[:, 0], mlp_gain, width) for r, i in zip(*held)]
        blocks += chunk
        rows = jnp.concatenate(chunk, axis=0)
        part = rows.shape[0] // n_section
        ordered = jnp.concatenate(relative(rows, q_order, c, part), axis=0)
        gate_keep, gate_send, up_keep, up_send = gate_up(ordered, gate_weight, up_weight)
        after = (
            gate_keep,
            swap(gate_send, "section", 1),
            up_keep,
            swap(up_send, "section", 1),
        )
    shares.append(after)

    own_sum = None
    for k, (gate_keep, gate_got, up_keep, up_got) in enumerate(shares):
        gate = halved(gate_keep + gate_got.astype(F32), "section", 1)
        up = halved(up_keep + up_got.astype(F32), "section", 1)
        units = (jax.nn.silu(gate) * up).astype(BF16)
        units = doubled(units, "section")
        hidden = jnp.zeros_like(units)
        for i, o in enumerate(q_order):
            piece = units[i * part : (i + 1) * part]
            hidden = lax.dynamic_update_slice_in_dim(hidden, piece, (c ^ o) * part, 0)
        update = jnp.dot(hidden, down_weight, preferred_element_type=F32)
        for i, j in enumerate(order[k * per : (k + 1) * per]):
            partial = halved(update[i * tok_local : (i + 1) * tok_local], "tensor")
            if j:
                partial = swap(partial.astype(BF16), "sample", j).astype(F32)
            own_sum = partial if own_sum is None else own_sum + partial

    updated = (mine[0].astype(F32) + own_sum).astype(BF16)
    out_values = updated.astype(F32)
    out_totals = butterfly(jnp.sum(out_values * out_values, axis=1), "section")

    mlp_rows = jnp.concatenate(blocks, axis=0)
    mlp_rows, hidden = lax.optimization_barrier((mlp_rows, hidden))
    mlp_columns = columns_of(mlp_rows, col_start, col_width, owners)
    mlp_cov = covariance(mlp_rows, mlp_columns, live, count)

    out_totals = doubled(out_totals[:, None], "tensor")
    attn_totals = gathered(out_totals)
    attn_raw = [doubled(x, "tensor") for x in gathered(updated)]
    hidden_out = jnp.zeros_like(hidden_in)
    for i, o in enumerate(t_order):
        piece = attn_raw[0][i * share : (i + 1) * share]
        hidden_out = lax.dynamic_update_slice_in_dim(hidden_out, piece, (t ^ o) * share, 0)
    attn_rows, attn_columns, after = [], [], ()
    for k in range(CHUNKS):
        held = (attn_raw[k * per : (k + 1) * per], attn_totals[k * per : (k + 1) * per])
        held, after = lax.optimization_barrier((held, after))
        if after:
            attn_rows.append(after[0])
        rows = jnp.concatenate(
            [normed(r, i[:, 0], attn_gain, width) for r, i in zip(*held)], axis=0
        )
        attn_columns.append(columns_of(rows, col_start, col_width, owners))
        after = (rows,)
    attn_rows = jnp.concatenate(attn_rows + [after[0]], axis=0)
    attn_columns = jnp.concatenate(attn_columns, axis=0)
    attn_live = [None] * n_sample
    for i, j in enumerate(order):
        attn_live[j] = live[i * tok_local : (i + 1) * tok_local]
    attn_live = jnp.concatenate(attn_live, axis=0)
    attn_cov = covariance(attn_rows, attn_columns, attn_live, count)
    return (hidden_out, mlp_cov, attn_cov)


def solution(mesh):
    in_specs = (
        P("sample", "section"),
        P("sample"),
        P("section"),
        P("section"),
        P(("sample", "tensor"), "section"),
        P(("sample", "tensor"), "section"),
        P(("sample", "tensor"), "section"),
    )
    out_specs = (
        P("sample", "section"),
        P("section", ("sample", "tensor")),
        P("section", ("sample", "tensor")),
    )
    return jax.shard_map(local, mesh=mesh, in_specs=in_specs, out_specs=out_specs, check_vma=False)
```

```python
import jax
import jax.numpy as jnp
from jax import lax
from jax.experimental import pallas as pl
from jax.experimental.pallas import tpu as pltpu
from jax.sharding import PartitionSpec as P

EPS = 1e-05
CHUNKS = 2
ROW_CONTRACT = (((1,), (1,)), ((), ()))
TOKEN_CONTRACT = (((0,), (0,)), ((), ()))
F32 = jnp.float32
BF16 = jnp.bfloat16


def swap(x, axis, d):
    return lax.ppermute(x, axis, [(i, i ^ d) for i in range(lax.axis_size(axis))])


def bits_up(axis):
    n, d, out = lax.axis_size(axis), 1, []
    while d < n:
        out.append(d)
        d *= 2
    return out


def offsets(axis):
    order = [0]
    for d in reversed(bits_up(axis)):
        order = order + [o ^ d for o in order]
    return order


def butterfly(x, axis):
    for d in bits_up(axis):
        x = x + swap(x, axis, d)
    return x


def doubled(x, axis):
    for d in reversed(bits_up(axis)):
        x = jnp.concatenate([x, swap(x, axis, d)], axis=0)
    return x


def halved(x, axis, skip=0):
    for d in bits_up(axis)[skip:]:
        half = x.shape[0] // 2
        x = x[:half] + swap(x[half:].astype(BF16), axis, d).astype(F32)
    return x


def gate_up_kernel(rows_ref, gate_ref, up_ref, gate_keep, gate_send, up_keep, up_send):
    half = gate_keep.shape[0]
    for weight, keep, send in ((gate_ref, gate_keep, gate_send), (up_ref, up_keep, up_send)):
        out = lax.dot_general(
            rows_ref[...], weight[...], ROW_CONTRACT, preferred_element_type=F32
        )
        keep[...] = out[:half]
        send[...] = out[half:].astype(BF16)


def gate_up(rows, gate_weight, up_weight):
    n, depth = rows.shape
    units = gate_weight.shape[0]
    tile = next((k for k in (512, 256, 128) if units % k == 0), units)
    half = n // 2
    weight_spec = pl.BlockSpec((tile, depth), lambda i: (i, 0))
    out_spec = pl.BlockSpec((half, tile), lambda i: (0, i))
    return pl.pallas_call(
        gate_up_kernel,
        grid=(units // tile,),
        in_specs=[pl.BlockSpec((n, depth), lambda i: (0, 0)), weight_spec, weight_spec],
        out_specs=[out_spec] * 4,
        out_shape=[
            jax.ShapeDtypeStruct((half, units), k) for k in (F32, BF16, F32, BF16)
        ],
        compiler_params=pltpu.CompilerParams(dimension_semantics=("arbitrary",)),
        cost_estimate=pl.CostEstimate(
            flops=4 * n * depth * units,
            bytes_accessed=4 * depth * units + 2 * n * depth + 6 * n * units,
            transcendentals=0,
        ),
    )(rows, gate_weight, up_weight)


def columns_of(rows, start, width, owners):
    names = ("sample", "tensor", "section")
    n_section = lax.axis_size("section")
    me = lax.axis_index("section")
    group = lax.axis_index("sample") * lax.axis_size("tensor") + lax.axis_index("tensor")
    owner = group * n_section // len(owners)
    value = lax.dynamic_slice_in_dim(rows, start, width, 1)
    have = [0]
    for d in reversed(bits_up("section")):
        pairs = [
            (g * n_section + (o ^ h), g * n_section + (o ^ h ^ d))
            for g, o in enumerate(owners)
            for h in have
        ]
        got = lax.ppermute(value, names, pairs)
        rel = me ^ owner
        takes = jnp.zeros((), jnp.bool_)
        for h in have:
            takes = takes | (rel == (h ^ d))
        value = jnp.where(takes, got, value)
        have = have + [h ^ d for h in have]
    return value


def normed(values, totals, gain, width):
    scales = lax.rsqrt(totals / width + EPS)
    return (values.astype(F32) * scales[:, None] * gain.astype(F32)).astype(BF16)


def covariance(rows_in, columns, live, count):
    weighted = rows_in * live[:, None]
    products = lax.dot_general(weighted, columns, TOKEN_CONTRACT, preferred_element_type=F32)
    row_means = jnp.dot(live, rows_in, preferred_element_type=F32) / count
    col_means = jnp.dot(live, columns, preferred_element_type=F32) / count
    return products / count - row_means[:, None] * col_means[None, :]


def local(hidden_in, token_ids, mlp_gain, attn_gain, gate_weight, up_weight, down_weight):
    n_sample = lax.axis_size("sample")
    n_tensor = lax.axis_size("tensor")
    n_section = lax.axis_size("section")
    tok_local, panel = hidden_in.shape
    width = panel * n_section
    share = tok_local // n_tensor
    groups = n_sample * n_tensor
    col_width = width // groups
    owners = [g * n_section // groups for g in range(groups)]
    t = lax.axis_index("tensor")
    c = lax.axis_index("section")
    group = lax.axis_index("sample") * n_tensor + t
    col_start = group * col_width - group * n_section // groups * panel
    t_order = offsets("tensor")
    q_order = offsets("section")

    def relative(x, order, me, size):
        return [lax.dynamic_slice_in_dim(x, (me ^ o) * size, size, 0) for o in order]

    values = hidden_in.astype(F32)
    totals = butterfly(jnp.sum(values * values, axis=1), "section")
    flags = jnp.stack([totals, (token_ids != 0).astype(F32)], axis=1)
    mine = relative(hidden_in, t_order, t, share)
    flags_mine = jnp.concatenate(relative(flags, t_order, t, share), axis=0)

    def gathered(x):
        out = [x]
        for j in range(1, n_sample):
            low = j & -j
            out.append(swap(out[j ^ low], "sample", low))
        return out

    order = list(range(0, n_sample, 2)) + list(range(1, n_sample, 2))
    info = gathered(flags_mine)
    raw = [jnp.concatenate(mine, axis=0)]
    raw += [doubled(r, "tensor") for r in gathered(mine[0])[1:]]
    raw = [raw[j] for j in order]
    info = [info[j] for j in order]
    live = jnp.concatenate([i[:, 1] for i in info], axis=0)
    count = jnp.sum(live)
    live = live.astype(BF16)

    per = n_sample // CHUNKS
    blocks, shares, after = [], [], ()
    for k in range(CHUNKS):
        held = (raw[k * per : (k + 1) * per], info[k * per : (k + 1) * per])
        held, after = lax.optimization_barrier((held, after))
        if after:
            shares.append(after)
        chunk = [normed(r, i[:, 0], mlp_gain, width) for r, i in zip(*held)]
        blocks += chunk
        rows = jnp.concatenate(chunk, axis=0)
        part = rows.shape[0] // n_section
        ordered = jnp.concatenate(relative(rows, q_order, c, part), axis=0)
        gate_keep, gate_send, up_keep, up_send = gate_up(ordered, gate_weight, up_weight)
        after = (
            gate_keep,
            swap(gate_send, "section", 1),
            up_keep,
            swap(up_send, "section", 1),
        )
    shares.append(after)

    own_sum = None
    for k, (gate_keep, gate_got, up_keep, up_got) in enumerate(shares):
        gate = halved(gate_keep + gate_got.astype(F32), "section", 1)
        up = halved(up_keep + up_got.astype(F32), "section", 1)
        units = (jax.nn.silu(gate) * up).astype(BF16)
        units = doubled(units, "section")
        hidden = jnp.zeros_like(units)
        for i, o in enumerate(q_order):
            piece = units[i * part : (i + 1) * part]
            hidden = lax.dynamic_update_slice_in_dim(hidden, piece, (c ^ o) * part, 0)
        update = jnp.dot(hidden, down_weight, preferred_element_type=F32)
        for i, j in enumerate(order[k * per : (k + 1) * per]):
            partial = halved(update[i * tok_local : (i + 1) * tok_local], "tensor")
            if j:
                partial = swap(partial.astype(BF16), "sample", j).astype(F32)
            own_sum = partial if own_sum is None else own_sum + partial

    updated = (mine[0].astype(F32) + own_sum).astype(BF16)
    out_values = updated.astype(F32)
    out_totals = butterfly(jnp.sum(out_values * out_values, axis=1), "section")

    mlp_rows = jnp.concatenate(blocks, axis=0)
    mlp_rows, hidden = lax.optimization_barrier((mlp_rows, hidden))
    mlp_columns = columns_of(mlp_rows, col_start, col_width, owners)
    mlp_cov = covariance(mlp_rows, mlp_columns, live, count)

    out_totals = doubled(out_totals[:, None], "tensor")
    attn_totals = gathered(out_totals)
    attn_raw = [doubled(x, "tensor") for x in gathered(updated)]
    hidden_out = jnp.zeros_like(hidden_in)
    for i, o in enumerate(t_order):
        piece = attn_raw[0][i * share : (i + 1) * share]
        hidden_out = lax.dynamic_update_slice_in_dim(hidden_out, piece, (t ^ o) * share, 0)
    attn_rows, attn_columns, after = [], [], ()
    for k in range(CHUNKS):
        held = (attn_raw[k * per : (k + 1) * per], attn_totals[k * per : (k + 1) * per])
        held, after = lax.optimization_barrier((held, after))
        if after:
            attn_rows.append(after[0])
        rows = jnp.concatenate(
            [normed(r, i[:, 0], attn_gain, width) for r, i in zip(*held)], axis=0
        )
        attn_columns.append(columns_of(rows, col_start, col_width, owners))
        after = (rows,)
    attn_rows = jnp.concatenate(attn_rows + [after[0]], axis=0)
    attn_columns = jnp.concatenate(attn_columns, axis=0)
    attn_live = [None] * n_sample
    for i, j in enumerate(order):
        attn_live[j] = live[i * tok_local : (i + 1) * tok_local]
    attn_live = jnp.concatenate(attn_live, axis=0)
    attn_cov = covariance(attn_rows, attn_columns, attn_live, count)
    return (hidden_out, mlp_cov, attn_cov)


def solution(mesh):
    in_specs = (
        P("sample", "section"),
        P("sample"),
        P("section"),
        P("section"),
        P(("sample", "tensor"), "section"),
        P(("sample", "tensor"), "section"),
        P(("sample", "tensor"), "section"),
    )
    out_specs = (
        P("sample", "section"),
        P("section", ("sample", "tensor")),
        P("section", ("sample", "tensor")),
    )
    return jax.shard_map(local, mesh=mesh, in_specs=in_specs, out_specs=out_specs, check_vma=False)
```
